512 devices in a mesh: batch: 64 (over z_lo, y, core), space: 8 (over x, z_hi).
Axes of the slice: x: 4, y: 4, z: 16 (z_hi: 2, z_lo: 8; z = z_hi * 8 + z_lo), core: 2. Of those that a mesh axis runs over, the one named last changes fastest.
Arguments:
- acts: bfloat16 [64, 32, 64, 640], P('batch', 'space'), may hold values from -6 to 6
- conv_weight: bfloat16 [5760, 640], P('batch', 'space'), may hold values from -0.078125 to 0.078125
- conv_bias: float32 [640], replicated, may hold values from -4 to 4
- out_cotangent: bfloat16 [64, 32, 64, 640], P('batch', 'space'), may hold values from -6 to 6
- basis_in: bfloat16 [5760, 64], P('batch'), may hold values from -0.078125 to 0.078125
- basis_out: bfloat16 [640, 64], P('batch'), may hold values from -0.25 to 0.25
- query_ids: int32 [8], replicated, may hold values from 0 to 63
Outputs:
- activated: bfloat16 [64, 32, 64, 640], P('batch', 'space')
- basis_in_new: bfloat16 [5760, 64], P('batch')
- scores: float32 [8, 64], P(None, 'batch')
The draws below stay inside these ranges and needn't reach their ends.
All inputs are finite; a program needn't handle non-finite values.
Results may differ from the reference program's by a relative error of at most 0.0031.
Values may be sent and summed in bfloat16 or wider, within the bound.
No kernel may reach another device: no remote copies, remote signals or barrier semaphores. Data moves between devices by JAX's collectives and lax.ppermute only.
A program may use at most 64 MiB of HBM per device.

```python
import math
import jax
import jax.numpy as jnp
from jax import lax

C = 640
WID = 64
RANK = 64
NQ = 8
PATCH = 5760
EXAMPLES = 64
HEIGHT = 32


def place_ends(entries, key, low, largest):
    shape = entries.shape
    spot = [jax.random.randint(jax.random.fold_in(key, axis), (), 0, shape[axis]) for axis in range(len(shape))]
    entries = entries.at[tuple(spot)].set(low)
    longest = shape.index(max(shape))
    spot[longest] = (spot[longest] + 1) % shape[longest]
    return entries.at[tuple(spot)].set(largest)


def steps_of(stream_key, shape, cuts, smallest, high):
    level, own = 1.0, jax.random.fold_in(stream_key, 6)
    for axis_at, blocks in cuts:
        heights = jnp.exp(jax.random.uniform(jax.random.fold_in(own, axis_at), (blocks,), jnp.float32, smallest / len(cuts), high / len(cuts)))
        level = level * jnp.repeat(heights, shape[axis_at] // blocks).reshape([-1 if axis == axis_at else 1 for axis in range(len(shape))])
    return level


def scatter_about(own_key, extent, width, limit, cuts=(), held_as=jnp.bfloat16):
    values = width * jax.random.normal(own_key, extent, jnp.float32)
    if cuts:
        values = values * steps_of(own_key, extent, cuts, -0.22, 0.18)
    return jnp.clip(values, -limit, limit).astype(held_as)


def setup_inputs(seed: int = 0) -> dict:
    streams_of = jax.random.split(jax.random.key(seed), 8)
    acts = scatter_about(streams_of[0], (EXAMPLES, HEIGHT, WID, C), 1.0, 6.0, ((0, 64), (1, 8)))
    conv_weight = scatter_about(streams_of[1], (PATCH, C), PATCH ** -0.5, 0.078125, ((0, 64), (1, 8)))
    conv_bias = scatter_about(streams_of[2], (C,), 0.7, 4.0, (), jnp.float32)
    out_cotangent = scatter_about(streams_of[3], (EXAMPLES, HEIGHT, WID, C), 1.0, 6.0, ((0, 64), (1, 8)))
    basis_in = scatter_about(streams_of[4], (PATCH, RANK), PATCH ** -0.5, 0.078125, ((0, 64),))
    basis_out = scatter_about(streams_of[5], (C, RANK), C ** -0.5, 0.25, ((0, 64),))
    query_ids = place_ends(jax.random.randint(streams_of[6], (NQ,), 0, EXAMPLES), jax.random.fold_in(streams_of[6], 1), 0, EXAMPLES - 1).astype(jnp.int32)
    return dict(acts=acts, conv_weight=conv_weight, conv_bias=conv_bias, out_cotangent=out_cotangent, basis_in=basis_in, basis_out=basis_out, query_ids=query_ids)


DAMPING = 0.1

def patches_of(latent):
    padded = jnp.pad(latent, ((1, 1), (1, 1), (0, 0)))
    rows_here = latent.shape[0]
    cols_here = latent.shape[1]
    shifted = [padded[row_shift:row_shift + rows_here, col_shift:col_shift + cols_here, :] for row_shift in range(3) for col_shift in range(3)]
    return jnp.stack(shifted, axis=2).reshape(rows_here * cols_here, 9 * latent.shape[2])

def reference(acts, conv_weight, conv_bias, out_cotangent, basis_in, basis_out, query_ids):
    channels = acts.shape[3]

    def first_pass(folded, inputs):
        latent, cotan = inputs
        patches = patches_of(latent)
        preact = jnp.dot(patches, conv_weight, preferred_element_type=jnp.float32) + conv_bias
        sigmoid_pre = jax.nn.sigmoid(preact)
        activated = (preact * sigmoid_pre).astype(jnp.bfloat16)
        grad_pre = (cotan.reshape(-1, channels).astype(jnp.float32) * sigmoid_pre * (1.0 + preact * (1.0 - sigmoid_pre))).astype(jnp.bfloat16)
        probe_in = jnp.dot(patches, basis_in, preferred_element_type=jnp.float32).astype(jnp.bfloat16)
        probe_out = jnp.dot(grad_pre, basis_out, preferred_element_type=jnp.float32).astype(jnp.bfloat16)
        term_in = jnp.dot(patches.T, probe_in, preferred_element_type=jnp.float32)
        term_out = jnp.dot(grad_pre.T, probe_out, preferred_element_type=jnp.float32)
        return ((folded[0] + term_in, folded[1] + term_out), (activated, grad_pre))
    start_in = jnp.zeros((PATCH, RANK), jnp.float32)
    start_out = jnp.zeros((C, RANK), jnp.float32)
    (sum_in, sum_out), (activated, grad_pre) = lax.scan(first_pass, (start_in, start_out), (acts, out_cotangent))
    positions = EXAMPLES * HEIGHT * WID
    basis_in_new = (sum_in / positions).astype(jnp.bfloat16)
    basis_out_new = (sum_out / positions).astype(jnp.bfloat16)
    scale_in = jnp.sqrt(lax.optimization_barrier(jnp.sum(jnp.square(basis_in_new.astype(jnp.float32)), axis=0)))
    scale_out = jnp.sqrt(lax.optimization_barrier(jnp.sum(jnp.square(basis_out_new.astype(jnp.float32)), axis=0)))

    def second_pass(inputs):
        latent, grads = inputs
        patches = patches_of(latent)
        feat_in = (jnp.dot(patches, basis_in_new, preferred_element_type=jnp.float32) / scale_in).astype(jnp.bfloat16)
        feat_out = (jnp.dot(grads, basis_out_new, preferred_element_type=jnp.float32) / scale_out).astype(jnp.bfloat16)
        return jnp.dot(feat_out.T, feat_in, preferred_element_type=jnp.float32) / HEIGHT
    projected = lax.map(second_pass, (acts, grad_pre))
    scaled = projected / (scale_out[:, None] * scale_in[None, :] + DAMPING)
    queries = jnp.take(projected, query_ids.astype(jnp.int32), axis=0)
    scores = jnp.einsum('qij,eij->qe', queries, scaled, precision=lax.Precision.HIGHEST) / (RANK * math.sqrt(RANK))
    activated = activated.reshape(acts.shape)
    return (activated, basis_in_new, scores)
```

```python
import math

import jax
import jax.numpy as jnp
from jax import lax
from jax.sharding import Mesh
from jax.sharding import PartitionSpec as P

DAMPING = 0.1
SPLIT = (("zl", 8), ("y", 4), ("c", 2), ("x", 4), ("zh", 2))
AXES = tuple(name for name, _ in SPLIT)
SIZES = dict(SPLIT)
BATCH = ("zl", "y", "c")
SPACE = ("x", "zh")
Z = ("zh", "zl")
F32, BF16 = jnp.float32, jnp.bfloat16

CH, RANK, TAPS = 640, 64, 9
PATCH = TAPS * CH
ROWS = PATCH // 64
COLS = CH // 8
WIDE = 768
SLOT = WIDE + 128


def exchange(value, axes):
    return lax.all_to_all(value, axes, 0, 0, tiled=True)


def gather(value, axes):
    count = math.prod(SIZES[a] for a in axes)
    copies = jnp.broadcast_to(value[None], (count,) + value.shape)
    return exchange(lax.optimization_barrier(copies), axes)


def halo(value):
    up = [(i, i + 1) for i in range(7)]
    down = [(j, i) for i, j in up]
    before = lax.ppermute(value[-1:], SPACE, up)
    after = lax.ppermute(value[:1], SPACE, down)
    return jnp.concatenate([before, value, after], axis=0)


def gather_weights(conv_weight, basis_in, basis_out):
    at = lax.axis_index(SPACE) * 8
    kernel = conv_weight.T
    basis = lax.dynamic_slice_in_dim(basis_in.T, at, 8, axis=0)
    outer = lax.dynamic_slice_in_dim(basis_out.T, at, 8, axis=0)
    rows = jnp.pad(jnp.concatenate([kernel, basis], axis=0), ((0, 0), (0, 128 - ROWS)))
    rows = lax.dynamic_update_slice(rows, outer, (COLS, ROWS))
    got = gather(rows, Z).reshape(2, 8, COLS + 8, 128)

    def merged(part, width):
        flat = part.transpose(0, 2, 1, 3).reshape(part.shape[0] * part.shape[2], -1)
        return jnp.pad(flat, ((0, 0), (0, WIDE - flat.shape[1])))

    joined = jnp.concatenate(
        [
            merged(got[:, :, :COLS, :ROWS], ROWS),
            merged(got[:, :, COLS:, :ROWS], ROWS),
            merged(got[:, :, COLS:, ROWS : ROWS + 10], 10),
        ],
        axis=0,
    )
    plane = gather(joined, ("y", "x"))
    both = gather(plane, ("c",)).reshape(2, 4, 4, 192, WIDE)
    weight = both[:, :, :, :160].reshape(8, CH, WIDE)
    inner = both[:, :, :, 160:176].reshape(8, RANK, WIDE)
    outer = both[:, :, :, 176:, :80].reshape(2, 4, RANK, 8, 10)
    outer = outer.transpose(2, 3, 1, 0, 4).reshape(RANK, CH)
    return weight, inner, outer


def dot_last(left, right):
    return lax.dot_general(left, right, (((1,), (1,)), ((), ())), preferred_element_type=F32)


def dot_first(left, right):
    return lax.dot_general(left, right, (((0,), (0,)), ((), ())), preferred_element_type=F32)


def reduced(term_in, term_out):
    outer = jnp.pad(term_out, ((0, 0), (0, 1024 - CH))).reshape(RANK, 8, 128).transpose(1, 0, 2)
    slots = jnp.concatenate([term_in, outer], axis=2).reshape(2, 4, RANK, SLOT)
    slots = exchange(slots, ("c",)).sum(0)
    part = slots.reshape(16, 16, SLOT)
    part = exchange(part, ("y", "x")).sum(0)
    part = exchange(part.reshape(16, SLOT // 128, 128), Z).sum(0)
    return part


def spread(part):
    part = gather(part, Z).reshape(16, SLOT)
    full = gather(part, ("c", "y", "x")).reshape(8, RANK, SLOT)
    inner = full[:, :, :WIDE]
    outer = full[:, :, WIDE:].transpose(1, 0, 2).reshape(RANK, 1024)[:, :CH]
    return inner, outer


def per_device(acts, conv_weight, conv_bias, out_cotangent, basis_in, basis_out, query_ids):
    positions = 256
    ext = jnp.pad(halo(acts[0]), ((0, 0), (1, 1), (0, 0)))
    weight, inner, outer = gather_weights(conv_weight, basis_in, basis_out)
    patches = jnp.stack(
        [ext[a : a + 4, b : b + 64] for a in range(3) for b in range(3)], axis=2
    ).reshape(positions, 8, 4, 2, ROWS)
    patches = patches.transpose(3, 2, 0, 1, 4).reshape(8, positions, 8 * ROWS)
    patches = jnp.pad(patches, ((0, 0), (0, 0), (0, WIDE - 8 * ROWS)))
    blocks = [patches[k] for k in range(8)]

    preact = sum(dot_last(blocks[k], weight[k]) for k in range(8)) + conv_bias
    sigmoid_pre = jax.nn.sigmoid(preact)
    activated = (preact * sigmoid_pre).astype(BF16).reshape(acts.shape)
    cot = out_cotangent.reshape(positions, CH).astype(F32)
    grad_pre = (cot * sigmoid_pre * (1.0 + preact * (1.0 - sigmoid_pre))).astype(BF16)
    probe_in = sum(dot_last(blocks[k], inner[k]) for k in range(8)).astype(BF16)
    probe_out = dot_last(grad_pre, outer).astype(BF16)
    term_in = jnp.stack([dot_first(probe_in, blocks[k]) for k in range(8)])
    term_out = dot_first(probe_out, grad_pre)

    total = 131072.0
    fresh = (reduced(term_in, term_out) / total).astype(BF16)
    new_in, new_out = spread(fresh)

    square_in = jnp.sum(jnp.square(new_in.astype(F32)), axis=(0, 2))
    square_out = jnp.sum(jnp.square(new_out.astype(F32)), axis=1)
    scale_in, scale_out = jnp.sqrt(square_in), jnp.sqrt(square_out)
    raw_in = sum(dot_last(blocks[k], new_in[k]) for k in range(8))
    raw_out = dot_last(grad_pre, new_out)
    feat_in = (raw_in / scale_in).astype(BF16)
    feat_out = (raw_out / scale_out).astype(BF16)
    partial = dot_first(feat_out, feat_in) / 32

    zl, y, c, x = (lax.axis_index(a) for a in ("zl", "y", "c", "x"))
    quarter = partial.reshape(4, 8, 128)
    sent = jnp.broadcast_to(quarter[None], (8, 4, 8, 128)).reshape(32, 8, 128)
    got = exchange(lax.optimization_barrier(sent), ("y", "c", "x"))
    near = got.reshape(8, 4, 8, 128).sum(1)
    every = gather(near, Z).reshape(2, 8, 8, 8, 128).sum(0).reshape(64, 8, 128)
    mine = lax.dynamic_index_in_dim(every, lax.axis_index(BATCH), axis=0, keepdims=False)
    scale = scale_out[:, None] * scale_in[None, :] + DAMPING
    scale = lax.dynamic_slice_in_dim(scale, x * 16, 16, axis=0).reshape(8, 128)
    queries = jnp.take(every, query_ids, axis=0)
    scores = jnp.sum(queries * (mine / scale)[None], axis=(1, 2)) / (RANK * math.sqrt(RANK))
    scores = jnp.broadcast_to(scores[:, None], (8, 128))
    scores = gather(scores, ("x",)).reshape(4, 8, 128).sum(0)[:, :1]

    row = lax.dynamic_index_in_dim(new_in, c * 4 + y, axis=0, keepdims=False)
    basis_in_new = lax.dynamic_slice_in_dim(row[:, : 8 * ROWS], zl * ROWS, ROWS, axis=1).T
    return (activated, basis_in_new, scores)


def solution(mesh):
    inner = Mesh(mesh.devices.reshape([n for _, n in SPLIT]), AXES)
    return jax.shard_map(
        per_device,
        mesh=inner,
        in_specs=(
            P(BATCH, SPACE, None, None),
            P(BATCH, SPACE),
            P(),
            P(BATCH, SPACE, None, None),
            P(BATCH, None),
            P(BATCH, None),
            P(),
        ),
        out_specs=(P(BATCH, SPACE, None, None), P(BATCH, None), P(None, BATCH)),
        check_vma=False,
    )
```

```python
import math

import jax
import jax.numpy as jnp
from jax import lax
from jax.experimental import pallas as pl
from jax.experimental.pallas import tpu as pltpu
from jax.sharding import Mesh
from jax.sharding import PartitionSpec as P

DAMPING = 0.1
SPLIT = (("zl", 8), ("y", 4), ("c", 2), ("x", 4), ("zh", 2))
AXES = tuple(name for name, _ in SPLIT)
SIZES = dict(SPLIT)
BATCH = ("zl", "y", "c")
SPACE = ("x", "zh")
Z = ("zh", "zl")
F32, BF16 = jnp.float32, jnp.bfloat16

CH, RANK, TAPS = 640, 64, 9
PATCH = TAPS * CH
ROWS = PATCH // 64
COLS = CH // 8
WIDE = 768
SLOT = WIDE + 128


def exchange(value, axes):
    return lax.all_to_all(value, axes, 0, 0, tiled=True)


def gather(value, axes):
    count = math.prod(SIZES[a] for a in axes)
    copies = jnp.broadcast_to(value[None], (count,) + value.shape)
    return exchange(lax.optimization_barrier(copies), axes)


def halo(value):
    up = [(i, i + 1) for i in range(7)]
    down = [(j, i) for i, j in up]
    return lax.ppermute(value[-1:], SPACE, up), lax.ppermute(value[:1], SPACE, down)


def gather_weights(conv_weight, basis_in, basis_out):
    at = lax.axis_index(SPACE) * 8
    kernel = conv_weight.T
    basis = lax.dynamic_slice_in_dim(basis_in.T, at, 8, axis=0)
    outer = lax.dynamic_slice_in_dim(basis_out.T, at, 8, axis=0)
    rows = jnp.pad(jnp.concatenate([kernel, basis], axis=0), ((0, 0), (0, 128 - ROWS)))
    rows = lax.dynamic_update_slice(rows, outer, (COLS, ROWS))
    got = gather(rows, Z).reshape(2, 8, COLS + 8, 128)

    def merged(part, width):
        flat = part.transpose(0, 2, 1, 3).reshape(part.shape[0] * part.shape[2], -1)
        return jnp.pad(flat, ((0, 0), (0, WIDE - flat.shape[1])))

    joined = jnp.concatenate(
        [
            merged(got[:, :, :COLS, :ROWS], ROWS),
            merged(got[:, :, COLS:, :ROWS], ROWS),
            merged(got[:, :, COLS:, ROWS : ROWS + 10], 10),
        ],
        axis=0,
    )
    return gather(joined, ("y", "x"))


def swap(value):
    return lax.ppermute(value, "c", [(0, 1), (1, 0)])


def dot_last(left, right):
    return lax.dot_general(left, right, (((1,), (1,)), ((), ())), preferred_element_type=F32)


def dot_plain(left, right):
    return jnp.dot(left, right, preferred_element_type=F32)


def vmem():
    return pl.BlockSpec(memory_space=pltpu.VMEM)


def patch_kernel(before, band, after, out, flat):
    row = lax.broadcasted_iota(jnp.int32, (64, CH), 0)
    for line in range(6):
        value = before[0] if line == 0 else after[0] if line == 5 else band[line - 1]
        wide = value.astype(F32)
        left = jnp.where(row == 0, 0.0, pltpu.roll(wide, 1, 0)).astype(BF16)
        right = jnp.where(row == 63, 0.0, pltpu.roll(wide, 63, 0)).astype(BF16)
        for tap_row in range(3):
            at = line - tap_row
            if 0 <= at < 4:
                for tap_col, moved in enumerate((left, value, right)):
                    tap = tap_row * 3 + tap_col
                    flat[at * 64 : at * 64 + 64, tap * CH : tap * CH + CH] = moved
    for c in range(2):
        for y in range(4):
            starts = [(zl * 8 + y * 2 + c) * ROWS for zl in range(8)]
            pieces = [flat[:, k : k + ROWS] for k in starts]
            pieces.append(jnp.zeros((256, WIDE - 8 * ROWS), BF16))
            out[c, y] = jnp.concatenate(pieces, axis=1)


def build_patches(before, band, after):
    return pl.pallas_call(
        patch_kernel,
        out_shape=jax.ShapeDtypeStruct((2, 4, 256, WIDE), BF16),
        in_specs=[vmem()] * 3,
        out_specs=vmem(),
        scratch_shapes=[pltpu.VMEM((256, PATCH), BF16)],
    )(before, band, after)


def first_kernel(
    core, own, other, patches, bias, cot, act, grad, kept, sent, total, outer, chunks
):
    y = pl.program_id(0)
    me = core[0]

    @pl.when(y == 0)
    def _():
        total[...] = jnp.zeros_like(total)
        outer[...] = jnp.zeros_like(outer)

    k = lax.broadcasted_iota(jnp.int32, (128, CH), 0)
    n = lax.broadcasted_iota(jnp.int32, (128, CH), 1)
    tens = lax.shift_right_logical(k * 6554, 16)
    spot = n - (tens * 80 + k - tens * 10)
    for c, half in ((me, own), (1 - me, other)):
        weight = half[...].reshape(WIDE, WIDE)
        total[...] += dot_last(patches[c, y], weight)
        piece = jnp.concatenate([half[x, 176:192, :128] for x in range(4)], axis=0)
        pick = jnp.where(spot == y * 20 + c * 10, 1.0, 0.0).astype(BF16)
        outer[...] += dot_plain(piece, pick)

    @pl.when(y == 3)
    def _():
        pre = jnp.concatenate([total[:, x * 192 : x * 192 + 160] for x in range(4)], axis=1)
        probe = jnp.concatenate(
            [total[:, x * 192 + 160 : x * 192 + 176] for x in range(4)], axis=1
        )
        pre = pre + bias[...]
        sig = jax.nn.sigmoid(pre)
        act[...] = (pre * sig).astype(BF16)
        slope = cot[...].astype(F32) * sig * (1.0 + pre * (1.0 - sig))
        grads = slope.astype(BF16)
        grad[...] = grads
        probe_in = probe.T.astype(BF16)
        probe_out = dot_last(outer[...].astype(BF16), grads).astype(BF16)
        term_out = dot_plain(probe_out, grads)
        for j in range(8):
            chunks[j] = term_out[:, j * 128 : j * 128 + 128] if j < 5 else jnp.zeros((RANK, 128), F32)
        for c, dest in ((me, kept), (1 - me, sent)):
            for at in range(4):
                dest[at, :, :WIDE] = dot_plain(probe_in, patches[c, at])
                dest[at, :, WIDE:] = chunks[c * 4 + at]


def first_pass(core, own, other, patches, bias, cot):
    half = pl.BlockSpec((4, 192, WIDE), lambda y, core: (y, 0, 0))

    def whole(*shape):
        return pl.BlockSpec(shape, lambda y, core: (0,) * len(shape))

    return pl.pallas_call(
        first_kernel,
        grid_spec=pltpu.PrefetchScalarGridSpec(
            num_scalar_prefetch=1,
            grid=(4,),
            in_specs=[half, half, whole(2, 4, 256, WIDE), whole(1, CH), whole(256, CH)],
            out_specs=[
                whole(256, CH),
                whole(256, CH),
                whole(4, RANK, SLOT),
                whole(4, RANK, SLOT),
            ],
            scratch_shapes=[
                pltpu.VMEM((256, WIDE), F32),
                pltpu.VMEM((RANK, CH), F32),
                pltpu.VMEM((8, RANK, 128), F32),
            ],
        ),
        out_shape=[
            jax.ShapeDtypeStruct((256, CH), BF16),
            jax.ShapeDtypeStruct((256, CH), BF16),
            jax.ShapeDtypeStruct((4, RANK, SLOT), F32),
            jax.ShapeDtypeStruct((4, RANK, SLOT), F32),
        ],
    )(core, own, other, patches, bias, cot)


def second_kernel(full, patches, grad, partial, scale_in, scale_out):
    raw_in = jnp.zeros((RANK, 256), F32)
    raw_out = jnp.zeros((RANK, 256), F32)
    square_in = jnp.zeros((RANK, 1), F32)
    square_out = jnp.zeros((RANK, 1), F32)
    for j in range(8):
        block = full[j, :, :WIDE]
        raw_in += dot_last(block, patches[j // 4, j % 4])
        square_in += jnp.sum(jnp.square(block.astype(F32)), axis=1, keepdims=True)
        if j < 5:
            chunk = full[j, :, WIDE:]
            raw_out += dot_last(chunk, grad[:, j * 128 : j * 128 + 128])
            square_out += jnp.sum(jnp.square(chunk.astype(F32)), axis=1, keepdims=True)
    root_in, root_out = jnp.sqrt(square_in), jnp.sqrt(square_out)
    feat_in = (raw_in / root_in).astype(BF16)
    feat_out = (raw_out / root_out).astype(BF16)
    partial[...] = dot_last(feat_out, feat_in) * (1.0 / 32)
    scale_in[...] = root_in
    scale_out[...] = root_out


def second_pass(full, patches, grad):
    return pl.pallas_call(
        second_kernel,
        out_shape=[
            jax.ShapeDtypeStruct((RANK, RANK), F32),
            jax.ShapeDtypeStruct((RANK, 1), F32),
            jax.ShapeDtypeStruct((RANK, 1), F32),
        ],
        in_specs=[vmem()] * 3,
        out_specs=[vmem()] * 3,
    )(full, patches, grad)


def reduced(kept, sent):
    part = (kept + swap(sent)).reshape(16, 16, SLOT)
    part = exchange(part, ("y", "x")).sum(0)
    return exchange(part.reshape(16, SLOT // 128, 128), Z).sum(0)


def spread(part):
    part = gather(part, Z).reshape(16, SLOT)
    return gather(part, ("c", "y", "x")).reshape(8, RANK, SLOT)


def per_device(acts, conv_weight, conv_bias, out_cotangent, basis_in, basis_out, query_ids):
    before, after = halo(acts[0])
    own = gather_weights(conv_weight, basis_in, basis_out)
    patches = build_patches(before, acts[0], after)
    core = lax.axis_index("c").astype(jnp.int32).reshape(1)
    activated, grad_pre, kept, sent = first_pass(
        core, own, swap(own), patches, conv_bias.reshape(1, CH), out_cotangent.reshape(256, CH)
    )
    activated = activated.reshape(acts.shape)
    full = spread((reduced(kept, sent) / 131072.0).astype(BF16))
    partial, scale_in, scale_out = second_pass(full, patches, grad_pre)

    zl, y, c, x = (lax.axis_index(a) for a in ("zl", "y", "c", "x"))
    quarter = partial.reshape(4, 8, 128)
    sent = jnp.broadcast_to(quarter[None], (8, 4, 8, 128)).reshape(32, 8, 128)
    got = exchange(lax.optimization_barrier(sent), ("y", "c", "x"))
    near = got.reshape(8, 4, 8, 128).sum(1)
    every = gather(near, Z).reshape(2, 8, 8, 8, 128).sum(0).reshape(64, 8, 128)
    mine = lax.dynamic_index_in_dim(every, lax.axis_index(BATCH), axis=0, keepdims=False)
    scale = scale_out * scale_in.T + DAMPING
    scale = lax.dynamic_slice_in_dim(scale, x * 16, 16, axis=0).reshape(8, 128)
    queries = jnp.take(every, query_ids, axis=0)
    scores = jnp.sum(queries * (mine / scale)[None], axis=(1, 2)) / (RANK * math.sqrt(RANK))
    scores = jnp.broadcast_to(scores[:, None], (8, 128))
    scores = gather(scores, ("x",)).reshape(4, 8, 128).sum(0)[:, :1]

    row = lax.dynamic_index_in_dim(full, c * 4 + y, axis=0, keepdims=False)
    basis_in_new = lax.dynamic_slice_in_dim(row[:, : 8 * ROWS], zl * ROWS, ROWS, axis=1).T
    return (activated, basis_in_new, scores)


def solution(mesh):
    inner = Mesh(mesh.devices.reshape([n for _, n in SPLIT]), AXES)
    return jax.shard_map(
        per_device,
        mesh=inner,
        in_specs=(
            P(BATCH, SPACE, None, None),
            P(BATCH, SPACE),
            P(),
            P(BATCH, SPACE, None, None),
            P(BATCH, None),
            P(BATCH, None),
            P(),
        ),
        out_specs=(P(BATCH, SPACE, None, None), P(BATCH, None), P(None, BATCH)),
        check_vma=False,
    )
```

```python
import math

import jax
import jax.numpy as jnp
from jax import lax
from jax.experimental import pallas as pl
from jax.experimental.pallas import tpu as pltpu
from jax.sharding import Mesh
from jax.sharding import PartitionSpec as P


DAMPING = 0.1
SPLIT = (("zl", 8), ("y", 4), ("c", 2), ("x", 4), ("zh", 2))
AXES = tuple(name for name, _ in SPLIT)
SIZES = dict(SPLIT)
BATCH = ("zl", "y", "c")
SPACE = ("x", "zh")
Z = ("zh", "zl")
F32, BF16 = jnp.float32, jnp.bfloat16

CH, RANK, TAPS = 640, 64, 9
PATCH = TAPS * CH
ROWS = PATCH // 64
COLS = CH // 8
WIDE = 768
SLOT = WIDE + 128


def exchange(value, axes):
    return lax.all_to_all(value, axes, 0, 0, tiled=True)


def gather(value, axes):
    count = math.prod(SIZES[a] for a in axes)
    copies = jnp.broadcast_to(value[None], (count,) + value.shape)
    return exchange(lax.optimization_barrier(copies), axes)


def halo(value):
    up = [(i, i + 1) for i in range(7)]
    down = [(j, i) for i, j in up]
    return lax.ppermute(value[-1:], SPACE, up), lax.ppermute(value[:1], SPACE, down)


def gather_weights(conv_weight, basis_in, basis_out):
    at = lax.axis_index(SPACE) * 8
    kernel = conv_weight.T
    basis = lax.dynamic_slice_in_dim(basis_in.T, at, 8, axis=0)
    outer = lax.dynamic_slice_in_dim(basis_out.T, at, 8, axis=0)
    rows = jnp.pad(jnp.concatenate([kernel, basis], axis=0), ((0, 0), (0, 128 - ROWS)))
    rows = lax.dynamic_update_slice(rows, outer, (COLS, ROWS))
    got = gather(rows, Z).reshape(2, 8, COLS + 8, 128)

    def merged(part):
        flat = part.transpose(0, 2, 1, 3).reshape(part.shape[0] * part.shape[2], -1)
        return jnp.pad(flat, ((0, 0), (0, WIDE - flat.shape[1])))

    joined = jnp.concatenate(
        [
            merged(got[:, :, :COLS, :ROWS]),
            merged(got[:, :, COLS:, :ROWS]),
            merged(got[:, :, COLS:, ROWS : ROWS + 10]),
        ],
        axis=0,
    )
    return gather(joined, ("y", "x"))


def swap(value):
    return lax.ppermute(value, "c", [(0, 1), (1, 0)])


def dot_last(left, right):
    return lax.dot_general(left, right, (((1,), (1,)), ((), ())), preferred_element_type=F32)


def dot_plain(left, right):
    return jnp.dot(left, right, preferred_element_type=F32)


def vmem():
    return pl.BlockSpec(memory_space=pltpu.VMEM)


def patch_kernel(before, band, after, out, flat):
    row = lax.broadcasted_iota(jnp.int32, (64, CH), 0)
    for line in range(6):
        value = before[0] if line == 0 else after[0] if line == 5 else band[line - 1]
        wide = value.astype(F32)
        left = jnp.where(row == 0, 0.0, pltpu.roll(wide, 1, 0)).astype(BF16)
        right = jnp.where(row == 63, 0.0, pltpu.roll(wide, 63, 0)).astype(BF16)
        for tap_row in range(3):
            at = line - tap_row
            if 0 <= at < 4:
                for tap_col, moved in enumerate((left, value, right)):
                    tap = tap_row * 3 + tap_col
                    flat[at * 64 : at * 64 + 64, tap * CH : tap * CH + CH] = moved
    for c in range(2):
        for y in range(4):
            starts = [(zl * 8 + y * 2 + c) * ROWS for zl in range(8)]
            pieces = [flat[:, k : k + ROWS] for k in starts]
            pieces.append(jnp.zeros((256, WIDE - 8 * ROWS), BF16))
            out[c, y] = jnp.concatenate(pieces, axis=1)


def build_patches(before, band, after):
    return pl.pallas_call(
        patch_kernel,
        out_shape=jax.ShapeDtypeStruct((2, 4, 256, WIDE), BF16),
        in_specs=[vmem()] * 3,
        out_specs=vmem(),
        scratch_shapes=[pltpu.VMEM((256, PATCH), BF16)],
    )(before, band, after)


def first_kernel(
    core, own, other, patches, bias, cot, act, grad, kept, sent, total, outer, chunks
):
    y = pl.program_id(0)
    me = core[0]

    @pl.when(y == 0)
    def _():
        total[...] = jnp.zeros_like(total)
        outer[...] = jnp.zeros_like(outer)

    k = lax.broadcasted_iota(jnp.int32, (128, CH), 0)
    n = lax.broadcasted_iota(jnp.int32, (128, CH), 1)
    tens = lax.shift_right_logical(k * 6554, 16)
    spot = n - (tens * 80 + k - tens * 10)
    for c, half in ((me, own), (1 - me, other)):
        weight = half[...].reshape(WIDE, WIDE)
        total[...] += dot_last(patches[c, y], weight)
        piece = jnp.concatenate([half[x, 176:192, :128] for x in range(4)], axis=0)
        pick = jnp.where(spot == y * 20 + c * 10, 1.0, 0.0).astype(BF16)
        outer[...] += dot_plain(piece, pick)

    @pl.when(y == 3)
    def _():
        pre = jnp.concatenate([total[:, x * 192 : x * 192 + 160] for x in range(4)], axis=1)
        probe = jnp.concatenate(
            [total[:, x * 192 + 160 : x * 192 + 176] for x in range(4)], axis=1
        )
        pre = pre + bias[...]
        sig = jax.nn.sigmoid(pre)
        act[...] = (pre * sig).astype(BF16)
        slope = cot[...].astype(F32) * sig * (1.0 + pre * (1.0 - sig))
        grads = slope.astype(BF16)
        grad[...] = grads
        probe_in = probe.T.astype(BF16)
        probe_out = dot_last(outer[...].astype(BF16), grads).astype(BF16)
        term_out = dot_plain(probe_out, grads)
        for j in range(8):
            chunks[j] = term_out[:, j * 128 : j * 128 + 128] if j < 5 else jnp.zeros((RANK, 128), F32)
        for c, dest in ((me, kept), (1 - me, sent)):
            for at in range(4):
                dest[at, :, :WIDE] = dot_plain(probe_in, patches[c, at])
                dest[at, :, WIDE:] = chunks[c * 4 + at]


def first_pass(core, own, other, patches, bias, cot):
    half = pl.BlockSpec((4, 192, WIDE), lambda y, core: (y, 0, 0))

    def whole(*shape):
        return pl.BlockSpec(shape, lambda y, core: (0,) * len(shape))

    return pl.pallas_call(
        first_kernel,
        grid_spec=pltpu.PrefetchScalarGridSpec(
            num_scalar_prefetch=1,
            grid=(4,),
            in_specs=[half, half, whole(2, 4, 256, WIDE), whole(1, CH), whole(256, CH)],
            out_specs=[
                whole(256, CH),
                whole(256, CH),
                whole(4, RANK, SLOT),
                whole(4, RANK, SLOT),
            ],
            scratch_shapes=[
                pltpu.VMEM((256, WIDE), F32),
                pltpu.VMEM((RANK, CH), F32),
                pltpu.VMEM((8, RANK, 128), F32),
            ],
        ),
        out_shape=[
            jax.ShapeDtypeStruct((256, CH), BF16),
            jax.ShapeDtypeStruct((256, CH), BF16),
            jax.ShapeDtypeStruct((4, RANK, SLOT), F32),
            jax.ShapeDtypeStruct((4, RANK, SLOT), F32),
        ],
    )(core, own, other, patches, bias, cot)


def second_kernel(core, own, other, patches, grad, partial, scale_in, scale_out):
    raw_in = jnp.zeros((RANK, 256), F32)
    raw_out = jnp.zeros((RANK, 256), F32)
    square_in = jnp.zeros((RANK, 1), F32)
    square_out = jnp.zeros((RANK, 1), F32)
    me = core[0]
    for c, half in ((me, own), (1 - me, other)):
        for y in range(4):
            block = half[y, :, :WIDE]
            raw_in += dot_last(block, patches[c, y])
            square_in += jnp.sum(jnp.square(block.astype(F32)), axis=1, keepdims=True)
            chunk = half[y, :, WIDE:]
            lane = pl.multiple_of(jnp.minimum(c * 4 + y, 4) * 128, 128)
            raw_out += dot_last(chunk, grad[:, pl.ds(lane, 128)])
            square_out += jnp.sum(jnp.square(chunk.astype(F32)), axis=1, keepdims=True)
    root_in, root_out = jnp.sqrt(square_in), jnp.sqrt(square_out)
    feat_in = (raw_in / root_in).astype(BF16)
    feat_out = (raw_out / root_out).astype(BF16)
    partial[...] = dot_last(feat_out, feat_in) * (1.0 / 32)
    scale_in[...] = root_in
    scale_out[...] = root_out


def second_pass(core, own, other, patches, grad):
    return pl.pallas_call(
        second_kernel,
        out_shape=[
            jax.ShapeDtypeStruct((RANK, RANK), F32),
            jax.ShapeDtypeStruct((RANK, 1), F32),
            jax.ShapeDtypeStruct((RANK, 1), F32),
        ],
        in_specs=[pl.BlockSpec(memory_space=pltpu.SMEM)] + [vmem()] * 4,
        out_specs=[vmem()] * 3,
    )(core, own, other, patches, grad)


def reduced(kept, sent):
    part = (kept + swap(sent)).reshape(16, 16, SLOT)
    part = exchange(part, ("y", "x")).sum(0)
    return exchange(part.reshape(16, SLOT // 128, 128), Z).sum(0)


def spread(part):
    part = gather(part, Z).reshape(16, SLOT)
    return gather(part, ("y", "x")).reshape(4, RANK, SLOT)


def per_device(acts, conv_weight, conv_bias, out_cotangent, basis_in, basis_out, query_ids):
    before, after = halo(acts[0])
    own = gather_weights(conv_weight, basis_in, basis_out)
    patches = build_patches(before, acts[0], after)
    core = lax.axis_index("c").astype(jnp.int32).reshape(1)
    activated, grad_pre, kept, sent = first_pass(
        core, own, swap(own), patches, conv_bias.reshape(1, CH), out_cotangent.reshape(256, CH)
    )
    activated = activated.reshape(acts.shape)
    fresh = spread((reduced(kept, sent) / 131072.0).astype(BF16))
    zl, y, c, x = (lax.axis_index(a) for a in ("zl", "y", "c", "x"))
    row = lax.dynamic_index_in_dim(fresh, y, axis=0, keepdims=False)
    basis_in_new = lax.dynamic_slice_in_dim(row[:, : 8 * ROWS], zl * ROWS, ROWS, axis=1).T
    partial, scale_in, scale_out = second_pass(core, fresh, swap(fresh), patches, grad_pre)

    scale = (scale_out * scale_in.T + DAMPING).reshape(32, 128)
    scale = lax.dynamic_slice_in_dim(scale, (y * 2 + c) * 4 + x, 1, axis=0)
    got = exchange(partial.reshape(32, 1, 128), ("y", "c", "x"))
    near = got.reshape(8, 4, 128).sum(1)
    every = gather(near, Z).reshape(2, 8, 8, 128).sum(0)
    mine = lax.dynamic_index_in_dim(every, zl, axis=0, keepdims=False) / scale
    queries = jnp.take(every.reshape(64, 128), query_ids, axis=0)
    pairs = jnp.sum(mine[:, None, :] * queries[None, :, :], axis=2)
    pairs = jnp.pad(pairs / (RANK * math.sqrt(RANK)), ((0, 0), (0, 120)))
    pairs = jnp.broadcast_to(pairs[:, None, None, :], (8, 4, 1, 128)).reshape(32, 1, 128)
    scores = exchange(lax.optimization_barrier(pairs), ("y", "c", "x")).sum(0)
    scores = scores[:, :8].T
    return (activated, basis_in_new, scores)


def solution(mesh):
    inner = Mesh(mesh.devices.reshape([n for _, n in SPLIT]), AXES)
    return jax.shard_map(
        per_device,
        mesh=inner,
        in_specs=(
            P(BATCH, SPACE, None, None),
            P(BATCH, SPACE),
            P(),
            P(BATCH, SPACE, None, None),
            P(BATCH, None),
            P(BATCH, None),
            P(),
        ),
        out_specs=(P(BATCH, SPACE, None, None), P(BATCH, None), P(None, BATCH)),
        check_vma=False,
    )
```
